32 devices in a mesh: dp: 4 (over y, x), rows: 4 (over z), cols: 2 (over core).
Axes of the slice: x: 2, y: 2, z: 4, core: 2. Of those that a mesh axis runs over, the one named last changes fastest.
Arguments:
- tokens_in: bfloat16 [1280, 8192], P('rows', ('dp', 'cols')), may hold values from -6 to 6
- segments: int32 [8, 1024], P('dp'), may hold values from 0 to 7, never falling along the last dimension, each value on 1 to 256 neighbouring positions
- query_weight: bfloat16 [1280, 1280], P('rows', 'cols'), may hold values from -0.15625 to 0.15625
- key_weight: bfloat16 [1280, 1280], P('rows', 'cols'), may hold values from -0.15625 to 0.15625
- value_weight: bfloat16 [1280, 1280], P('rows', 'cols'), may hold values from -0.15625 to 0.15625
- output_weight: bfloat16 [1280, 1280], P('cols', 'rows'), may hold values from -1.25 to 1.25
- hidden_weight: bfloat16 [1280, 1280], P('rows', 'cols'), may hold values from -0.15625 to 0.15625
- hidden_bias: float32 [1280], P('cols'), may hold values from -3 to 3
- final_weight: bfloat16 [1280, 1280], P('cols', 'rows'), may hold values from -0.15625 to 0.15625
- final_bias: float32 [1280], P('rows'), may hold values from -3 to 3
- attention_gain: float32 [1280], P('rows'), may hold values from 0.1 to 1.9
- feed_gain: float32 [1280], P('rows'), may hold values from 0.1 to 1.9
- query_scale: float32 [80], replicated, may hold values from -2.5 to 2.5
- clip_limit: float32 [16], P('cols'), may hold values from 3 to 12
- cotangent: bfloat16 [1280, 8192], P('rows', ('dp', 'cols')), may hold values from -6 to 6
Outputs:
- layer_output: bfloat16 [1280, 8192], P('rows', ('dp', 'cols'))
- input_gradient: float32 [1280, 8192], P('rows', ('dp', 'cols'))
- query_gradient: float32 [1280, 1280], P('rows', 'cols')
- key_gradient: float32 [1280, 1280], P('rows', 'cols')
- value_gradient: float32 [1280, 1280], P('rows', 'cols')
- output_gradient: float32 [1280, 1280], P('cols', 'rows')
- hidden_gradient: float32 [1280, 1280], P('rows', 'cols')
- hidden_bias_gradient: float32 [1280], P('cols')
- final_gradient: float32 [1280, 1280], P('cols', 'rows')
- final_bias_gradient: float32 [1280], P('rows')
- attention_gain_gradient: float32 [1280], P('rows')
- feed_gain_gradient: float32 [1280], P('rows')
- query_scale_gradient: float32 [80], replicated
- head_max: float32 [16], P('cols')
- clipped_query: float32 [1280, 1280], P('rows', 'cols')
- clipped_key: float32 [1280, 1280], P('rows', 'cols')
The draws below stay inside these ranges and needn't reach their ends.
Inputs may be any that keep to these rules, and one draw needn't show every extreme that they name: `segments`: along each sequence the segment numbers never fall; each segment covers 1 to 256 positions, and one covers exactly 256.
All inputs are finite; a program needn't handle non-finite values.
Results may differ from the reference program's by a relative error of at most 0.015.
Values may be sent and summed in bfloat16 or wider, within the bound.
No kernel may reach another device: no remote copies, remote signals or barrier semaphores. Data moves between devices by JAX's collectives and lax.ppermute only.
A program may use at most 128 MiB of HBM per device.

```python
import math
from functools import partial
import jax
import jax.numpy as jnp
import numpy as np
from jax import lax

D = 1280
HEADS = 16
HDIM = 80
FF = 1280
LEN = 1024
PATCH = 256
HD = 1280
SEQS = 8
TOKENS = 8192
SEGS = 8


def block_scale(rng, dims, pieces, least, largest):
    factor_of, own = 1.0, jax.random.fold_in(rng, 6)
    for dim, blocks in pieces:
        steps = jnp.exp(jax.random.uniform(jax.random.fold_in(own, dim), (blocks,), jnp.float32, least / len(pieces), largest / len(pieces)))
        factor_of = factor_of * jnp.repeat(steps, dims[dim] // blocks).reshape([-1 if axis == dim else 1 for axis in range(len(dims))])
    return factor_of


def split_up(amount, total, bound, lean):
    loads = [(1 << 20) // math.isqrt(standing ** lean) + 1 for standing in range(2, amount + 1)]
    surplus, given = total - bound - (amount - 1), [1] * (amount - 1)
    while surplus > 0:
        free = [i for i in range(amount - 1) if given[i] < bound]
        pool, remaining = sum([loads[i] for i in free]), surplus
        for i in free:
            more = min(bound - given[i], max(1, remaining * loads[i] // pool), surplus)
            given[i] = given[i] + more
            surplus = surplus - more
    return np.array([bound] + given)


def uneven_parts(rng, number_of, total, bound, slope):
    if number_of == 2:
        one = jax.random.randint(rng, (), max(1, total - bound), min(bound, total - 1) + 1)
        return jnp.stack([one, total - one])
    sizes = jnp.asarray(split_up(number_of, total, bound, slope), jnp.int32)
    couples = (number_of - 1) // 2
    source_of, receiver = sizes[1:1 + 2 * couples:2], sizes[2:2 + 2 * couples:2]
    slack = jnp.minimum(source_of - 1, bound - receiver)
    moved = jax.random.randint(jax.random.fold_in(rng, 1), (couples,), 0, 1 << 20) % (slack + 1)
    sizes = sizes.at[1:1 + 2 * couples:2].set(source_of - moved).at[2:2 + 2 * couples:2].set(receiver + moved)
    return sizes[jax.random.permutation(jax.random.fold_in(rng, 2), number_of)]


def bell_draw(stream_key, extent, scale, reach, shards=(), kind=jnp.bfloat16):
    values = jax.random.normal(stream_key, extent, jnp.float32) * scale
    if len(shards) > 0:
        values = block_scale(stream_key, extent, shards, -0.22, 0.18) * values
    return jnp.clip(values, min=-reach, max=reach).astype(kind)


def setup_inputs(seed: int = 0) -> dict:
    seeds = jax.random.split(jax.random.key(seed), 16)
    tokens_in = bell_draw(seeds[0], (D, TOKENS), 1.0, 6.0, ((0, 4), (1, 8)))
    segments = jax.vmap(lambda own: jnp.searchsorted(jnp.cumsum(uneven_parts(own, SEGS, LEN, PATCH, 1)), jnp.arange(LEN), side="right"))(jax.random.split(seeds[1], SEQS)).reshape((SEQS, LEN)).astype(jnp.int32)
    query_weight = bell_draw(seeds[2], (D, HD), D ** -0.5, 0.15625, ((0, 4), (1, 2)))
    key_weight = bell_draw(seeds[3], (D, HD), D ** -0.5, 0.15625, ((0, 4), (1, 2)))
    value_weight = bell_draw(seeds[4], (D, HD), D ** -0.5, 0.15625, ((0, 4), (1, 2)))
    output_weight = bell_draw(seeds[5], (HD, D), (HDIM // 4) ** -0.5, 1.25, ((0, 2), (1, 4)))
    hidden_weight = bell_draw(seeds[6], (D, FF), D ** -0.5, 0.15625, ((0, 4), (1, 2)))
    hidden_bias = bell_draw(seeds[7], (FF,), 0.5, 3.0, ((0, 2),), jnp.float32)
    final_weight = bell_draw(seeds[8], (FF, D), FF ** -0.5, 0.15625, ((0, 2), (1, 4)))
    final_bias = bell_draw(seeds[9], (D,), 0.5, 3.0, ((0, 4),), jnp.float32)
    attention_gain = jnp.clip(1.0 + 0.18 * jax.random.normal(seeds[10], (D,), jnp.float32), 0.1, 1.9)
    feed_gain = jnp.clip(1.0 + 0.18 * jax.random.normal(seeds[11], (D,), jnp.float32), 0.1, 1.9)
    query_scale = bell_draw(seeds[12], (HDIM,), 0.5, 2.5, (), jnp.float32)
    clip_limit = jnp.clip(jnp.exp(math.log(12.0) - 1.3862944 * jax.random.uniform(seeds[13], (HEADS,), jnp.float32) ** block_scale(seeds[13], (HEADS,), ((0, 2),), -0.2, 0.2)), 3.0, 12.0)
    cotangent = bell_draw(seeds[14], (D, TOKENS), 1.0, 6.0, ((0, 4), (1, 8)))
    return dict(tokens_in=tokens_in, segments=segments, query_weight=query_weight, key_weight=key_weight, value_weight=value_weight, output_weight=output_weight, hidden_weight=hidden_weight, hidden_bias=hidden_bias, final_weight=final_weight, final_bias=final_bias, attention_gain=attention_gain, feed_gain=feed_gain, query_scale=query_scale, clip_limit=clip_limit, cotangent=cotangent)


EPSILON = 1e-06
NEGATIVE = -1e+30
LOG2E = 1.442695
HIGHEST = lax.Precision.HIGHEST

@jax.custom_vjp
def low(v):
    return lax.optimization_barrier(v.astype(jnp.bfloat16)).astype(jnp.float32)

@jax.custom_vjp
def low_back(v):
    return v

def low_keep(v):
    return (low(v), None)

def low_pass(kept, grad):
    return (grad,)

def back_keep(v):
    return (v, None)

def back_low(kept, grad):
    return (low(grad),)
low.defvjp(low_keep, low_pass)
low_back.defvjp(back_keep, back_low)

def matmul(left_side, right_side):
    return jnp.dot(left_side, right_side, preferred_element_type=jnp.float32, precision=HIGHEST)

def normalize(array_in, gain):
    return array_in * lax.rsqrt(lax.optimization_barrier(jnp.mean(array_in * array_in, axis=1, keepdims=True)) + EPSILON) * gain

def attend(head_items):
    query_seq, key_seq, value_seq, seg_ids = head_items
    position = jnp.arange(LEN, dtype=jnp.int32)
    visible = (position[None, :] <= position[:, None]) | (seg_ids[None, :] == seg_ids[:, None])
    scores = low_back(jnp.einsum('qhd,khd->hqk', query_seq, key_seq, precision=HIGHEST))
    masked = jnp.where(visible[None], scores, NEGATIVE)
    row_top = lax.optimization_barrier(jnp.max(masked, axis=2))
    exponent = jnp.exp(masked - row_top[:, :, None])
    weights = exponent / lax.optimization_barrier(jnp.sum(exponent, axis=2, keepdims=True))
    mixed = jnp.einsum('hqk,khd->qhd', low(weights), value_seq, precision=HIGHEST)
    return (low(low_back(mixed)), lax.optimization_barrier(jnp.max(row_top, axis=1)))

def forward(segments, inputs, query_w, key_w, value_w, output_w, hidden_w, hidden_b, final_w, final_b, gain_one, gain_two, scale_raw):
    normed_one = low(normalize(inputs, gain_one))
    query_raw = low_back(matmul(normed_one, query_w))
    keys_all = low(low_back(matmul(normed_one, key_w)))
    values_all = low(low_back(matmul(normed_one, value_w)))
    scale_row = LOG2E / math.sqrt(HDIM) * jax.nn.softplus(scale_raw)
    queries = low(query_raw.reshape(TOKENS, HEADS, HDIM) * scale_row)
    mixed, tops = lax.map(jax.checkpoint(attend), (queries.reshape(SEQS, LEN, HEADS, HDIM), keys_all.reshape(SEQS, LEN, HEADS, HDIM), values_all.reshape(SEQS, LEN, HEADS, HDIM), segments))
    mixed = mixed.reshape(TOKENS, HEADS * HDIM)
    residual = inputs + low_back(matmul(mixed, output_w))
    normed_two = low(normalize(residual, gain_two))
    pre_act = low_back(matmul(normed_two, hidden_w) + hidden_b)
    activated = low(jax.nn.silu(pre_act))
    result = residual + low_back(matmul(activated, final_w) + final_b)
    return (result, lax.optimization_barrier(jnp.max(tops, axis=0)))

def reference(tokens_in, segments, query_weight, key_weight, value_weight, output_weight, hidden_weight, hidden_bias, final_weight, final_bias, attention_gain, feed_gain, query_scale, clip_limit, cotangent):
    inputs = tokens_in.astype(jnp.float32).T
    query_w = query_weight.astype(jnp.float32)
    key_w = key_weight.astype(jnp.float32)
    value_w = value_weight.astype(jnp.float32)
    output_w = output_weight.astype(jnp.float32)
    hidden_w = hidden_weight.astype(jnp.float32)
    final_w = final_weight.astype(jnp.float32)
    result, pullback, tops = jax.vjp(partial(forward, segments), inputs, query_w, key_w, value_w, output_w, hidden_w, hidden_bias, final_w, final_bias, attention_gain, feed_gain, query_scale, has_aux=True)
    grads = pullback(cotangent.astype(jnp.float32).T)
    factor = jnp.repeat(jnp.sqrt(clip_limit / jnp.maximum(tops, clip_limit)), HDIM)
    return (result.T.astype(jnp.bfloat16), grads[0].T, grads[1], grads[2], grads[3], grads[4], grads[5], grads[6], grads[7], grads[8], grads[9], grads[10], grads[11], tops, query_w * factor[None, :], key_w * factor[None, :])
```

```python
import functools
import math

import jax
import jax.numpy as jnp
from jax import lax
from jax.experimental import pallas as pl
from jax.experimental.pallas import tpu as pltpu
from jax.sharding import PartitionSpec as P

EPSILON = 1e-06
NEGATIVE = -1e30
LOG2E = 1.442695
PATCH = 256
BF = jnp.bfloat16
F32 = jnp.float32
RC = ("rows", "cols")


def dot_nn(a, b):
    return lax.dot_general(a, b, (((1,), (0,)), ((), ())), preferred_element_type=F32)


def dot_nt(a, b):
    return lax.dot_general(a, b, (((1,), (1,)), ((), ())), preferred_element_type=F32)


def dot_tn(a, b):
    return lax.dot_general(a, b, (((0,), (0,)), ((), ())), preferred_element_type=F32)


def pick(blocks, index):
    return lax.dynamic_index_in_dim(blocks, index, 0, keepdims=False)


def put(blocks, part, index):
    return lax.dynamic_update_index_in_dim(blocks, part, index, 0)


def swap_cols(array_in):
    return lax.ppermute(array_in, "cols", [(0, 1), (1, 0)])


def exchange(blocks, axis, count, position, groups=1):
    out = blocks
    for k in range(1, count):
        perm = [(g * count + i, g * count + (i ^ k)) for g in range(groups) for i in range(count)]
        part = lax.ppermute(pick(blocks, position ^ k), axis, perm)
        out = put(out, part, position ^ k)
    return out


def gather(part, axis, count, position):
    out = jnp.zeros((count,) + part.shape, part.dtype)
    out = put(out, part, position)
    for k in range(1, count):
        perm = [(i, i ^ k) for i in range(count)]
        out = put(out, lax.ppermute(part, axis, perm), position ^ k)
    return out


def total(blocks):
    return jnp.sum(blocks.astype(F32), axis=0)


def butterfly(value, combine, sizes):
    for axis, count in sizes:
        step = 1
        while step < count:
            other = lax.ppermute(value, axis, [(i, i ^ step) for i in range(count)])
            value = combine(value, other)
            step *= 2
    return value


def visible_bias(bias_ref, seg_row_ref, seg_col_ref, nb, width, reach):
    for ib in range(nb):
        span = min(nb, ib + 1 + reach) - ib
        rows = span * width
        key_pos = ib * width + lax.broadcasted_iota(jnp.int32, (rows, width), 0)
        query_pos = ib * width + lax.broadcasted_iota(jnp.int32, (rows, width), 1)
        seg_keys = seg_col_ref[pl.ds(ib * width, rows), :]
        seg_query = seg_row_ref[ib]
        ok = (key_pos <= query_pos) | (seg_keys == seg_query)
        bias_ref[ib, pl.ds(0, rows), :] = jnp.where(ok, 0.0, NEGATIVE)


def attend_kernel(nb, width, reach, seg_row_ref, seg_col_ref, q_ref, k_ref, v_ref, o_ref, lse_ref, top_ref, bias_ref):
    @pl.when(pl.program_id(0) == 0)
    def _():
        visible_bias(bias_ref, seg_row_ref, seg_col_ref, nb, width, reach)

    keys = [k_ref[j].T for j in range(nb)]
    for ib in range(nb):
        query = q_ref[ib]
        last = min(nb, ib + 1 + reach)
        scores = []
        for j in range(last):
            part = dot_nn(keys[j], query)
            if j >= ib:
                part = part + bias_ref[ib, pl.ds((j - ib) * width, width), :]
            scores.append(part)
        top = functools.reduce(jnp.maximum, [jnp.max(s, axis=0, keepdims=True) for s in scores])
        denom = jnp.zeros((1, width), F32)
        out = jnp.zeros(query.shape, F32)
        for j in range(last):
            weight = jnp.exp(scores[j] - top)
            denom = denom + jnp.sum(weight, axis=0, keepdims=True)
            out = out + dot_nn(v_ref[j], weight.astype(BF))
        o_ref[ib] = (out / denom).astype(BF)
        lse_ref[0, ib] = top + jnp.log(denom)
        top_ref[0, ib] = top


def attend_back_kernel(
    nb, width, reach, seg_row_ref, seg_col_ref, q_ref, k_ref, v_ref, g_ref, o_ref, lse_ref, raw_ref, scale_ref,
    dq_ref, dk_ref, dv_ref, part_ref, bias_ref, acc_k, acc_v,
):
    @pl.when(pl.program_id(0) == 0)
    def _():
        visible_bias(bias_ref, seg_row_ref, seg_col_ref, nb, width, reach)

    keys = [k_ref[j].T for j in range(nb)]
    values = [v_ref[j].T for j in range(nb)]
    acc_k[...] = jnp.zeros_like(acc_k)
    acc_v[...] = jnp.zeros_like(acc_v)
    scale_part = jnp.zeros(part_ref.shape[1:], F32)
    for ib in range(nb):
        query = q_ref[ib]
        grad = g_ref[ib]
        last = min(nb, ib + 1 + reach)
        lse = lse_ref[0, ib]
        delta = jnp.sum(grad.astype(F32) * o_ref[ib].astype(F32), axis=0, keepdims=True)
        dq = jnp.zeros(query.shape, F32)
        for j in range(last):
            part = dot_nn(keys[j], query)
            if j >= ib:
                part = part + bias_ref[ib, pl.ds((j - ib) * width, width), :]
            weight = jnp.exp(part - lse)
            prob_grad = dot_nn(values[j], grad)
            score_grad = (weight * (prob_grad - delta)).astype(BF)
            acc_v[j] += dot_nt(grad, weight.astype(BF))
            acc_k[j] += dot_nt(query, score_grad)
            dq = dq + dot_nn(k_ref[j], score_grad)
        scale_part = scale_part + dq * raw_ref[ib]
        dq_ref[ib] = (dq * scale_ref[...]).astype(BF)
    part_ref[0] = scale_part
    dk_ref[...] = acc_k[...].astype(BF)
    dv_ref[...] = acc_v[...].astype(BF)


def attention_calls(nb, width, heads, head_dim, seq_len):
    reach = (width - 1 + PATCH - 1) // width
    whole = pl.BlockSpec((nb, 1, width), lambda h: (0, 0, 0))
    column = pl.BlockSpec((seq_len, 1), lambda h: (0, 0))

    def head(offset):
        return pl.BlockSpec((nb, head_dim, width), lambda h: (0, offset * heads + h, 0))

    stat = pl.BlockSpec((1, nb, 1, width), lambda h: (h, 0, 0, 0))
    stat_shape = jax.ShapeDtypeStruct((heads, nb, 1, width), F32)
    act_shape = jax.ShapeDtypeStruct((nb, heads * head_dim, width), BF)
    bias = pltpu.VMEM((nb, min(nb, 1 + reach) * width, width), F32)
    params = pltpu.CompilerParams(vmem_limit_bytes=60000 * 1024)
    unit = heads * seq_len * seq_len
    forward = pl.pallas_call(
        functools.partial(attend_kernel, nb, width, reach),
        grid=(heads,),
        in_specs=[whole, column, head(0), head(1), head(2)],
        out_specs=[head(0), stat, stat],
        out_shape=[act_shape, stat_shape, stat_shape],
        scratch_shapes=[bias],
        compiler_params=params,
        cost_estimate=pl.CostEstimate(flops=unit * 1024, transcendentals=unit, bytes_accessed=4 * act_shape.size),
        name="attend",
    )
    backward = pl.pallas_call(
        functools.partial(attend_back_kernel, nb, width, reach),
        grid=(heads,),
        in_specs=[
            whole, column, head(0), head(1), head(2), head(0), head(0), stat, head(0),
            pl.BlockSpec((head_dim, 1), lambda h: (0, 0)),
        ],
        out_specs=[head(0), head(0), head(0), pl.BlockSpec((1, head_dim, width), lambda h: (h, 0, 0))],
        out_shape=[act_shape, act_shape, act_shape, jax.ShapeDtypeStruct((heads, head_dim, width), F32)],
        scratch_shapes=[bias, pltpu.VMEM((nb, head_dim, width), F32), pltpu.VMEM((nb, head_dim, width), F32)],
        compiler_params=params,
        cost_estimate=pl.CostEstimate(flops=unit * 2560, transcendentals=unit, bytes_accessed=10 * act_shape.size),
        name="attend_back",
    )
    return forward, backward


def shards(
    tokens_in, segments, query_weight, key_weight, value_weight, output_weight, hidden_weight, hidden_bias,
    final_weight, final_bias, attention_gain, feed_gain, query_scale, clip_limit, cotangent,
):
    rows, cols, quarters = lax.axis_size("rows"), lax.axis_size("cols"), lax.axis_size("dp")
    half = rows // 2
    feat = tokens_in.shape[0]
    width = feat * rows
    seq_len = segments.shape[1]
    head_dim = query_scale.shape[0]
    head_cols = query_weight.shape[1]
    block = head_cols * cols // rows
    heads = block // head_dim
    toks = seq_len // rows
    dp_at, row_at, col_at = lax.axis_index("dp"), lax.axis_index("rows"), lax.axis_index("cols")
    pair = row_at // half
    spot = (row_at % half) * cols + col_at
    mine = col_at == pair

    def blocked(array_in):
        return array_in.reshape(array_in.shape[0], rows, toks).transpose(1, 0, 2)

    def unblocked(array_in):
        return array_in.transpose(1, 0, 2).reshape(array_in.shape[1], rows * toks)

    x_blocks = blocked(tokens_in)
    g_blocks = blocked(cotangent)

    sub = head_cols // half
    qkv_quarter = jnp.stack([w.reshape(quarters, feat // quarters, half, sub) for w in (query_weight, key_weight, value_weight)])
    qkv_mine = lax.dynamic_index_in_dim(qkv_quarter, dp_at, 1, keepdims=False)
    qkv_send = qkv_mine.transpose(2, 1, 0, 3).reshape(half, feat // quarters, 3 * sub)
    qkv_rows = jnp.zeros((rows, feat // quarters, 3 * sub), BF)
    for k in range(rows):
        perm = [
            (r * cols + c, ((r ^ k) // half) * rows + c * half + (r ^ k) % half)
            for r in range(rows)
            for c in range(cols)
        ]
        part = lax.ppermute(pick(qkv_send, (row_at ^ k) % half), RC, perm)
        qkv_rows = put(qkv_rows, part, (pair * half + spot % half) ^ k)
    qkv_all = gather(qkv_rows, "dp", quarters, dp_at)
    joined_weight = qkv_all.transpose(1, 0, 2, 3).reshape(width, 3 * sub)

    small = jnp.stack([attention_gain, feed_gain, final_bias])
    small = gather(small, "rows", rows, row_at).transpose(1, 0, 2).reshape(3, width)
    gain_one, gain_two, bias_two = small[0][:, None], small[1][:, None], small[2][:, None]
    bias_one = put(jnp.zeros((cols, head_cols), F32), hidden_bias, col_at)
    bias_one = put(bias_one, swap_cols(hidden_bias), 1 - col_at).reshape(-1)[:, None]

    x_parts = []
    for k in range(rows):
        if k == 0:
            part = jnp.where(mine, x_blocks, jnp.zeros_like(x_blocks))
        else:
            perm = [
                ((r ^ k) * cols + c, r * cols + c) for c in range(cols) for r in range(c * half, (c + 1) * half)
            ]
            part = lax.ppermute(x_blocks, RC, perm)
        x_parts.append(part + swap_cols(part))
    x_all = jnp.zeros((rows,) + x_blocks.shape, BF)
    for k in range(rows):
        x_all = put(x_all, x_parts[k], row_at ^ k)
    x_all = x_all.transpose(1, 0, 2, 3).reshape(rows, width, toks)

    def whole_rows(weight):
        own = lax.dynamic_index_in_dim(weight.reshape(quarters, feat // quarters, head_cols), dp_at, 0, keepdims=False)
        by_row = gather(own, "rows", rows, row_at)
        every = gather(by_row, "dp", quarters, dp_at)
        every = every.transpose(1, 0, 2, 3).reshape(width, head_cols)
        both = put(jnp.zeros((cols, width, head_cols), BF), every, col_at)
        both = put(both, swap_cols(every), 1 - col_at)
        return both.transpose(1, 0, 2).reshape(width, cols * head_cols)

    def whole_cols(weight):
        own = pick(weight.reshape(quarters, head_cols // quarters, feat), dp_at)
        by_row = gather(own, "rows", rows, row_at)
        by_row = by_row.transpose(1, 0, 2).reshape(head_cols // quarters, width)
        every = gather(by_row, "dp", quarters, dp_at).reshape(head_cols, width)
        both = put(jnp.zeros((cols, head_cols, width), BF), every, col_at)
        both = put(both, swap_cols(every), 1 - col_at)
        return both.reshape(cols * head_cols, width)

    out_weight = whole_cols(output_weight)
    hid_weight = whole_rows(hidden_weight)
    fin_weight = whole_cols(final_weight)

    g_tok = jnp.zeros((rows, feat, toks), BF)
    for k in range(rows):
        perm = [(r * cols + c, c * rows + (r ^ k)) for r in range(rows) for c in range(cols)]
        part = lax.ppermute(pick(g_blocks, row_at ^ k), RC, perm)
        g_tok = put(g_tok, part, spot ^ k)
    g_tok = g_tok.reshape(width, toks)

    x32 = x_all.astype(F32)
    inv_all = lax.rsqrt(jnp.sum(x32 * x32, axis=1, keepdims=True) / width + EPSILON)
    normed_one = (x32 * inv_all * gain_one[None]).astype(BF)
    normed_flat = unblocked(normed_one)
    qkv = dot_tn(joined_weight, normed_flat)
    scale_col = (LOG2E / math.sqrt(head_dim) * jax.nn.softplus(query_scale))[:, None]
    qkv_tok = blocked(qkv)
    query_raw = qkv_tok[:, :block]
    query_bf = (query_raw * jnp.tile(scale_col, (heads, 1))[None]).astype(BF)
    qkv_bf = jnp.concatenate([query_bf, qkv_tok[:, block:].astype(BF)], axis=1)
    seg_own = lax.dynamic_index_in_dim(segments, pair, 0, keepdims=False)

    nb = 4 if seq_len % 1024 == 0 else rows
    attn_width = seq_len // nb

    def to_attn(a):
        if nb == rows:
            return a
        return unblocked(a).reshape(a.shape[1], nb, attn_width).transpose(1, 0, 2)

    def from_attn(a):
        if nb == rows:
            return a
        return blocked(a.transpose(1, 0, 2).reshape(a.shape[1], seq_len))

    forward, backward = attention_calls(nb, attn_width, heads, head_dim, seq_len)
    seg_row, seg_col = seg_own.reshape(nb, 1, attn_width), seg_own[:, None]
    qkv_bf = to_attn(qkv_bf)
    query_raw = to_attn(query_raw)
    mixed_attn, lse, tops = forward(seg_row, seg_col, qkv_bf, qkv_bf, qkv_bf)

    mixed = exchange(from_attn(mixed_attn), RC, rows, spot, groups=cols).reshape(width, toks)

    inputs = pick(x_all, spot).astype(F32)
    inv_one = pick(inv_all, spot)
    residual = inputs + dot_tn(out_weight, mixed)
    inv_two = lax.rsqrt(jnp.sum(residual * residual, axis=0, keepdims=True) / width + EPSILON)
    normed_two = (residual * inv_two * gain_two).astype(BF)
    pre_act = dot_tn(hid_weight, normed_two) + bias_one
    sigmoid_pre = jax.nn.sigmoid(pre_act)
    activated = (pre_act * sigmoid_pre).astype(BF)
    output_tok = (residual + dot_tn(fin_weight, activated) + bias_two).astype(BF)
    grad_out = g_tok.astype(F32)
    act_grad = dot_nn(fin_weight, g_tok)
    pre_grad = (act_grad * sigmoid_pre * (1.0 + pre_act * (1.0 - sigmoid_pre))).astype(BF)
    two_grad = dot_nn(hid_weight, pre_grad)
    scaled_two = two_grad * gain_two
    dot_two = jnp.sum(scaled_two * residual, axis=0, keepdims=True)
    residual_grad = grad_out + inv_two * scaled_two - residual * inv_two**3 * (dot_two / width)
    branch_grad = residual_grad.astype(BF)
    mix_grad = dot_nn(out_weight, branch_grad).astype(BF)
    gain_two_part = jnp.sum(two_grad * residual * inv_two, axis=1)
    bias_one_part = jnp.sum(pre_grad.astype(F32), axis=1)

    mix_heads = exchange(mix_grad.reshape(rows, block, toks), RC, rows, spot, groups=cols)
    dq, dk, dv, scale_part = backward(
        seg_row, seg_col, qkv_bf, qkv_bf, qkv_bf, to_attn(mix_heads), mixed_attn, lse, query_raw, scale_col
    )
    joined_flat = jnp.concatenate([unblocked(from_attn(d)) for d in (dq, dk, dv)], axis=0)

    one_part = dot_nn(joined_weight, joined_flat).astype(BF)
    one_part = blocked(one_part)
    if rows > 1:
        one_part = one_part.reshape(half, cols, width, toks)
        keep = lax.dynamic_index_in_dim(one_part, col_at, 1, keepdims=False).astype(F32)
        give = lax.dynamic_index_in_dim(one_part, 1 - col_at, 1, keepdims=False)
        chip_part = (keep + swap_cols(give).astype(F32)).astype(BF)
    spot_row = row_at % half
    one_grad = jnp.zeros((width, toks), F32)
    for k in range(half):
        if k == 0:
            part = pick(chip_part, spot_row)
        else:
            perm = [(r, (r // half) * half + ((r % half) ^ k)) for r in range(rows)]
            part = lax.ppermute(pick(chip_part, spot_row ^ k), "rows", perm)
        one_grad = one_grad + part.astype(F32)
    scaled_one = one_grad * gain_one
    dot_one = jnp.sum(scaled_one * inputs, axis=0, keepdims=True)
    input_tok = residual_grad + inv_one * scaled_one - inputs * inv_one**3 * (dot_one / width)
    gain_one_part = jnp.sum(one_grad * inputs * inv_one, axis=1)

    def to_features(array_in):
        blocks = array_in.reshape(rows, feat, toks)
        out = jnp.zeros((rows, feat, toks), BF)
        for k in range(rows):
            perm = [(p * rows + h, (h ^ k) * cols + p) for p in range(cols) for h in range(rows)]
            part = lax.ppermute(pick(blocks, spot ^ k), RC, perm)
            out = put(out, part, row_at ^ k)
        return unblocked(out)

    layer_output = to_features(output_tok)
    input_gradient = to_features(input_tok.astype(BF)).astype(F32)

    def halves(array_in):
        parts = array_in.reshape(cols, head_cols, toks)
        return jnp.concatenate([pick(parts, col_at), swap_cols(pick(parts, 1 - col_at))], axis=1)

    def both(array_in):
        return jnp.concatenate([array_in, swap_cols(array_in)], axis=1)

    def reduce_cols(partial):
        parts = partial.astype(BF).reshape(quarters, head_cols // quarters, width)
        own = total(exchange(parts, "dp", quarters, dp_at)).astype(BF)
        own = own.reshape(head_cols // quarters, rows, feat).transpose(1, 0, 2)
        own = total(exchange(own, "rows", rows, row_at)).astype(BF)
        return gather(own, "dp", quarters, dp_at).reshape(head_cols, feat).astype(F32)

    def by_quarter(partial):
        return partial.astype(BF).reshape(rows, quarters, feat // quarters, -1).transpose(1, 0, 2, 3)

    def reduce_rows(partial):
        own = total(exchange(by_quarter(partial), "dp", quarters, dp_at)).astype(BF)
        own = total(exchange(own, "rows", rows, row_at)).astype(BF)
        return gather(own, "dp", quarters, dp_at).reshape(feat, head_cols).astype(F32)

    final_grad = reduce_cols(dot_nt(halves(activated), both(g_tok)))
    hidden_grad = reduce_rows(dot_nt(both(normed_two), halves(pre_grad)))
    output_grad = reduce_cols(dot_nt(halves(mixed), both(branch_grad)))

    joined_grad = dot_nt(normed_flat, joined_flat)
    own = total(exchange(by_quarter(joined_grad), "dp", quarters, dp_at)).astype(BF)
    gathered = jnp.zeros_like(own)
    source = pair * half + spot % half
    for k in range(rows):
        perm = [
            (p * rows + h, ((p * half + h % half) ^ k) * cols + h // half) for p in range(cols) for h in range(rows)
        ]
        part = lax.ppermute(pick(own, source ^ k), RC, perm)
        gathered = put(gathered, part, row_at ^ k)
    own = total(gathered.reshape(cols, half, feat // quarters, 3, block))
    own = own.astype(BF).transpose(1, 2, 0, 3).reshape(feat // quarters, 3 * head_cols)
    joined_sum = gather(own, "dp", quarters, dp_at).reshape(feat, 3 * head_cols).astype(F32)

    every = (("cols", cols), ("rows", rows), ("dp", quarters))
    packed = jnp.concatenate([gain_one_part, gain_two_part, bias_one_part, jnp.sum(scale_part, axis=(0, 2))])
    packed = butterfly(packed, jnp.add, every)

    def own_block(vector, count, index):
        return pick(vector.reshape(count, -1), index)

    gain_one_sum = own_block(packed[:width], rows, row_at)
    gain_two_sum = own_block(packed[width : 2 * width], rows, row_at)
    bias_one_sum = own_block(packed[2 * width : 3 * width], cols, col_at)
    scale_sum = packed[3 * width :]
    bias_two_sum = butterfly(
        jnp.sum(cotangent.astype(F32), axis=1), jnp.add, (("cols", cols), ("dp", quarters))
    )
    scale_gradient = scale_sum * (LOG2E / math.sqrt(head_dim)) * jax.nn.sigmoid(query_scale)

    head_top = jnp.max(tops, axis=(1, 2, 3))
    top_all = put(jnp.full((rows, heads), NEGATIVE, F32), head_top, spot)
    top_all = butterfly(top_all, jnp.maximum, every).reshape(cols, -1)
    top_heads = pick(top_all, col_at)
    factor = jnp.repeat(jnp.sqrt(clip_limit / jnp.maximum(top_heads, clip_limit)), head_dim)
    clipped_query = query_weight.astype(F32) * factor[None, :]
    clipped_key = key_weight.astype(F32) * factor[None, :]
    return (
        layer_output,
        input_gradient,
        joined_sum[:, :head_cols],
        joined_sum[:, head_cols : 2 * head_cols],
        joined_sum[:, 2 * head_cols :],
        output_grad,
        hidden_grad,
        bias_one_sum,
        final_grad,
        bias_two_sum,
        gain_one_sum,
        gain_two_sum,
        scale_gradient,
        top_heads,
        clipped_query,
        clipped_key,
    )


def at(ref, *index):
    return ref[index]


def ds16(start, size):
    return pl.ds(pl.multiple_of(start, 16), size)


def ds128(start, size):
    return pl.ds(pl.multiple_of(start, 128), size)


def head_block(spot):
    return (spot % 2) * 2 + spot // 2


def local_call(kernel, outs, scratch, name, flops=1 << 20, moved=1 << 20, operands=None, spaces=None):
    vmem = pl.BlockSpec(memory_space=pltpu.VMEM)
    spaces = spaces or {}
    specs = [pl.BlockSpec(memory_space=pltpu.SMEM)] + [
        pl.BlockSpec(memory_space=spaces[i]) if i in spaces else vmem for i in range(1, operands)
    ]
    return pl.pallas_call(
        kernel,
        in_specs=specs,
        out_specs=[vmem] * len(outs),
        out_shape=[jax.ShapeDtypeStruct(s, t) for s, t in outs],
        scratch_shapes=scratch,
        compiler_params=pltpu.CompilerParams(vmem_limit_bytes=60000 * 1024),
        cost_estimate=pl.CostEstimate(flops=flops, transcendentals=0, bytes_accessed=moved),
        name=name,
    )


def pack_kernel(
    at_ref, q_ref, k_ref, v_ref, h_ref, o_ref, f_ref, one_ref, two_ref, bias_ref, g_ref,
    even_ref, odd_ref, feed_ref, g_even_ref, g_odd_ref, col_s, turn_s,
):
    dp, row = at_ref[0], at_ref[1]
    same = row % 2 == 0
    feat, wide = q_ref.shape
    quarter, sub = feat // 4, wide // 2
    rows = ds16(dp * quarter, quarter)
    pieces = []
    for ref in (one_ref, two_ref, bias_ref):
        value = ref[...]
        high = value.astype(BF).astype(F32)
        middle = (value - high).astype(BF).astype(F32)
        pieces += [high, middle, value - high - middle]
    extra = even_ref.shape[1] - 3 * sub
    pieces.append(jnp.zeros((extra - len(pieces), feat), F32))
    col_s[...] = jnp.concatenate(pieces, axis=0).T
    columns = col_s[rows, :].astype(BF)
    weights = [ref[rows, :] for ref in (q_ref, k_ref, v_ref)]
    first = jnp.concatenate([w[:, :sub] for w in weights] + [columns], axis=1)
    second = jnp.concatenate([w[:, sub:] for w in weights] + [columns], axis=1)
    even_ref[...] = jnp.where(same, first, second)
    odd_ref[...] = jnp.where(same, second, first)
    feed_ref[0] = h_ref[rows, :]
    for i, ref in ((1, o_ref), (2, f_ref)):
        turn_s[...] = ref[...].T
        feed_ref[i] = turn_s[rows, :]
    span = g_ref.shape[1] // 2
    g_even_ref[...] = g_ref[:, ds128((row % 2) * span, span)]
    g_odd_ref[...] = g_ref[:, ds128((1 - row % 2) * span, span)]


def project_kernel(
    at_ref, x0, x1, x2, x3, s0, s1, s2, s3, w0, w1, w2, w3, scale_ref,
    qkv_ref, raw_ref, normed_ref, weight_ref, col_ref, x_tok_ref, inv_tok_ref, x_s, turn_s,
):
    dp, row, col = at_ref[0], at_ref[1], at_ref[2]
    pair, spot = row // 2, (row % 2) * 2 + col
    feat, seq = x0.shape
    width = 4 * feat
    quarter = feat // 4
    joined = qkv_ref.shape[1]
    block = joined // 3
    toks = seq // 4
    heads = block // scale_ref.shape[0]
    for k, (own, other) in enumerate(((x0, s0), (x1, s1), (x2, s2), (x3, s3))):
        rows = ds16((row ^ k) * feat, feat)

        @pl.when(col == pair)
        def _(own=own, rows=rows):
            x_s[rows, :] = own[...]

        @pl.when(col != pair)
        def _(other=other, rows=rows):
            x_s[rows, :] = other[...]

    for m, part in enumerate((w0, w1, w2, w3)):
        for k in range(4):
            weight_ref[ds16((row ^ k) * feat + (dp ^ m) * quarter, quarter), :] = part[k]
    cols = weight_ref[:, joined:].astype(F32)
    vectors = [cols[:, 3 * i : 3 * i + 1] + cols[:, 3 * i + 1 : 3 * i + 2] + cols[:, 3 * i + 2 : 3 * i + 3] for i in range(3)]
    lane = lax.broadcasted_iota(jnp.int32, col_ref.shape, 1)
    col_ref[...] = jnp.where(lane == 0, vectors[0], jnp.where(lane == 1, vectors[1], vectors[2]))
    turn_s[...] = weight_ref[:, :joined].T
    scale = jnp.concatenate([scale_ref[...]] * heads, axis=0)
    gain = vectors[0]
    for i in range(4):
        lanes = pl.ds(i * toks, toks)
        x = x_s[:, lanes].astype(F32)
        inv = lax.rsqrt(jnp.sum(x * x, axis=0, keepdims=True) / width + EPSILON)
        normed = (x * inv * gain).astype(BF)
        normed_ref[:, lanes] = normed
        out = dot_nn(turn_s[...], normed)
        raw_ref[i] = out[:block]
        qkv_ref[i, :block, :] = (out[:block] * scale).astype(BF)
        qkv_ref[i, block:, :] = out[block:].astype(BF)
    mine = x_s[:, ds128(spot * toks, toks)]
    x_tok_ref[...] = mine
    mine = mine.astype(F32)
    inv_tok_ref[...] = lax.rsqrt(jnp.sum(mine * mine, axis=0, keepdims=True) / width + EPSILON)


def attend_fast_kernel(
    nb, width, reach, at_ref, seg_row_ref, seg_col_ref, q_ref, k_ref, v_ref,
    o_ref, d0, d1, d2, d3, lse_ref, top_ref, bias_ref,
):
    @pl.when(pl.program_id(0) == 0)
    def _():
        visible_bias(bias_ref, seg_row_ref, seg_col_ref, nb, width, reach)

    spot = (at_ref[1] % 2) * 2 + at_ref[2]
    keys = [k_ref[j].T for j in range(nb)]
    for ib in range(nb):
        query = q_ref[ib]
        last = min(nb, ib + 1 + reach)
        scores = []
        for j in range(last):
            part = dot_nn(keys[j], query)
            if j >= ib:
                part = part + bias_ref[ib, pl.ds((j - ib) * width, width), :]
            scores.append(part)
        top = functools.reduce(jnp.maximum, [jnp.max(s, axis=0, keepdims=True) for s in scores])
        denom = jnp.zeros((1, width), F32)
        out = jnp.zeros(query.shape, F32)
        for j in range(last):
            weight = jnp.exp(scores[j] - top)
            denom = denom + jnp.sum(weight, axis=0, keepdims=True)
            out = out + dot_nn(v_ref[j], weight.astype(BF))
        o_ref[ib] = (out / denom).astype(BF)
        lse_ref[0, ib] = top + jnp.log(denom)
        top_ref[0, ib] = top
    for k, ref in enumerate((d0, d1, d2, d3)):
        ref[...] = o_ref[spot ^ k]


def middle_kernel(
    at_ref, x_ref, m0, m1, m2, m3, z0, z1, z2, z3, y0, y1, y2, y3, col_ref, bias_ref,
    a0, a1, a2, a3, b0, b1, b2, b3,
    e0, e1, e2, e3, h0, h1, h2, h3, rest_ref, common_ref, keep_ref, send_ref, sums_ref,
    w_s, mixed_s, g_s, act_s, pre_s, flat_s, sem,
):
    dp, row, col = at_ref[0], at_ref[1], at_ref[2]
    pair, spot = row // 2, (row % 2) * 2 + col
    width, toks = x_ref.shape
    feat, half = width // 4, width // 2
    quarter = feat // 4
    copies = {}
    for w in (1, 0, 2):
        for m, (own, other) in enumerate(((a0, b0), (a1, b1), (a2, b2), (a3, b3))):
            for k in range(4):
                rows = ds16((row ^ k) * feat + (dp ^ m) * quarter, quarter)
                for s, (src, side) in enumerate(((own, col), (other, 1 - col))):
                    copies[w, m, k, s] = pltpu.make_async_copy(
                        src.at[k, w],
                        w_s.at[w, rows, ds128(side * half, half)],
                        sem.at[((w * 4 + m) * 4 + k) * 2 + s],
                    )
                    copies[w, m, k, s].start()

    def arrive(w):
        for key, copy in copies.items():
            if key[0] == w:
                copy.wait()

    for k, part in enumerate((m0, m1, m2, m3)):
        mixed_s[ds16(head_block(spot ^ k) * feat, feat), :] = part[...]
    for k, (own, other) in enumerate(((z0, y0), (z1, y1), (z2, y2), (z3, y3))):
        rows = ds16((row ^ k) * feat, feat)

        @pl.when(col == pair)
        def _(own=own, rows=rows):
            g_s[rows, :] = own[:, ds128(col * toks, toks)]

        @pl.when(col != pair)
        def _(other=other, rows=rows):
            g_s[rows, :] = other[:, ds128(col * toks, toks)]

    gain, bias_out = col_ref[:, 1:2], col_ref[:, 2:3]
    arrive(1)
    residual = x_ref[...].astype(F32) + dot_nn(w_s[1], mixed_s[...])
    inv = lax.rsqrt(jnp.sum(residual * residual, axis=0, keepdims=True) / width + EPSILON)
    normed = (residual * inv * gain).astype(BF)
    common_ref[:width] = normed
    arrive(0)
    pre = (dot_nn(normed.T, w_s[0]) + bias_ref[...]).T
    sig = 1.0 / (1.0 + jnp.exp(-pre))
    act = (pre * sig).astype(BF)
    act_s[...] = act
    arrive(2)
    flat_s[...] = (residual + dot_nn(w_s[2], act) + bias_out).astype(BF)
    for k, ref in enumerate((e0, e1, e2, e3)):
        ref[...] = flat_s[ds16((spot ^ k) * feat, feat), :]
    g_bf = g_s[...]
    common_ref[2 * width :] = g_bf
    grad = g_bf.astype(F32)
    act_grad = dot_nn(g_bf.T, w_s[2]).T
    pre_grad = (act_grad * sig * (1.0 + pre * (1.0 - sig))).astype(BF)
    pre_s[...] = pre_grad
    two_grad = dot_nn(w_s[0], pre_grad)
    scaled = two_grad * gain
    dots = jnp.sum(scaled * residual, axis=0, keepdims=True)
    rest = grad + inv * scaled - residual * (inv * inv * inv * (dots / width))
    rest_ref[...] = rest
    branch = rest.astype(BF)
    common_ref[width : 2 * width] = branch
    flat_s[...] = dot_nn(branch.T, w_s[1]).T.astype(BF)
    for k, ref in enumerate((h0, h1, h2, h3)):
        ref[...] = flat_s[ds16(head_block(spot ^ k) * feat, feat), :]
    for i, source in enumerate((act_s, pre_s, mixed_s)):
        keep_ref[pl.ds(i * half, half), :] = source[ds16(col * half, half), :]
        send_ref[pl.ds(i * half, half), :] = source[ds16((1 - col) * half, half), :]
    lane = lax.broadcasted_iota(jnp.int32, sums_ref.shape, 1)
    gain_part = jnp.sum(two_grad * residual * inv, axis=1, keepdims=True)
    hidden_part = jnp.sum(pre_grad.astype(F32), axis=1, keepdims=True)
    bias_part = jnp.sum(grad, axis=1, keepdims=True)
    sums_ref[...] = jnp.where(lane == 0, gain_part, jnp.where(lane == 1, hidden_part, bias_part))


def attend_back_fast_kernel(
    nb, width, reach, at_ref, seg_row_ref, seg_col_ref, q_ref, k_ref, v_ref, g0, g1, g2, g3, o_ref, lse_ref, raw_ref,
    scale_ref, dq_ref, dk_ref, dv_ref, part_ref, bias_ref, acc_k, acc_v, g_s,
):
    spot = (at_ref[1] % 2) * 2 + at_ref[2]
    for k, ref in enumerate((g0, g1, g2, g3)):
        g_s[spot ^ k] = ref[...]
    attend_back_kernel(
        nb, width, reach, seg_row_ref, seg_col_ref, q_ref, k_ref, v_ref, g_s, o_ref, lse_ref, raw_ref, scale_ref,
        dq_ref, dk_ref, dv_ref, part_ref, bias_ref, acc_k, acc_v,
    )


def spread_kernel(at_ref, weight_ref, dq_ref, dk_ref, dv_ref, give_far, give_near, keep_far, keep_near, join_s):
    row, col = at_ref[1], at_ref[2]
    block = dq_ref.shape[1]
    for i, j, ref in ((1, 1, give_far), (0, 1, give_near), (1, 0, keep_far), (0, 0, keep_near)):
        tok = ((row % 2) ^ i) * 2 + (col ^ j)
        for n, part in enumerate((dq_ref, dk_ref, dv_ref)):
            join_s[pl.ds(n * block, block), :] = part[tok]
        ref[...] = dot_nn(weight_ref[:, : 3 * block], join_s[...]).astype(BF)


def input_kernel(
    at_ref, near_ref, chip_ref, far_ref, x_ref, inv_ref, rest_ref, col_ref, e0, e1, e2, e3, sums_ref, flat_s
):
    spot = (at_ref[1] % 2) * 2 + at_ref[2]
    width = x_ref.shape[0]
    feat = width // 4
    one = near_ref[...].astype(F32) + chip_ref[...].astype(F32) + far_ref[...].astype(F32)
    x = x_ref[...].astype(F32)
    inv = inv_ref[...]
    scaled = one * col_ref[:, 0:1]
    dots = jnp.sum(scaled * x, axis=0, keepdims=True)
    flat_s[...] = (rest_ref[...] + inv * scaled - x * (inv * inv * inv * (dots / width))).astype(BF)
    for k, ref in enumerate((e0, e1, e2, e3)):
        ref[...] = flat_s[ds16((spot ^ k) * feat, feat), :]
    part = jnp.sum(one * x * inv, axis=1, keepdims=True)
    sums_ref[...] = jnp.broadcast_to(part, sums_ref.shape)


def place_kernel(at_ref, p0, p1, p2, p3, out_ref):
    toks = p0.shape[1]
    for k, ref in enumerate((p0, p1, p2, p3)):
        out_ref[:, ds128((at_ref[1] ^ k) * toks, toks)] = ref[...].astype(out_ref.dtype)


def joined_kernel(at_ref, normed_ref, dq_ref, dk_ref, dv_ref, o0, o1, o2, o3, join_s, part_s):
    dp = at_ref[0]
    block, toks = dq_ref.shape[1:]
    feat = normed_ref.shape[0] // 4
    quarter = feat // 4
    for n, part in enumerate((dq_ref, dk_ref, dv_ref)):
        for i in range(4):
            join_s[pl.ds(n * block, block), pl.ds(i * toks, toks)] = part[i]
    for r in range(4):
        part_s[...] = dot_nt(normed_ref[pl.ds(r * feat, feat), :], join_s[...]).astype(BF)
        for k, ref in enumerate((o0, o1, o2, o3)):
            ref[r] = part_s[ds16((dp ^ k) * quarter, quarter), :]


def feed_kernel(at_ref, own_ref, got_ref, keep_ref, half_ref, o0, o1, o2, o3, a_s, b_s, part_s):
    dp = at_ref[0]
    toks = own_ref.shape[1]
    width = own_ref.shape[0] // 3
    feat, half = width // 4, width // 2
    quarter = feat // 4
    for w, (i, j) in enumerate(((0, 1), (1, 2), (2, 0))):
        for n, (wide, slim) in enumerate(((own_ref, keep_ref), (got_ref, half_ref))):
            a_s[:, pl.ds(n * toks, toks)] = wide[pl.ds(i * width, width), :]
            b_s[:, pl.ds(n * toks, toks)] = slim[pl.ds(j * half, half), :]
        part_s[...] = dot_nt(a_s[...], b_s[...]).astype(BF)
        for r in range(4):
            for k, ref in enumerate((o0, o1, o2, o3)):
                ref[w, r] = part_s[ds16(r * feat + (dp ^ k) * quarter, quarter), :]


def feed_sum_kernel(at_ref, p0, p1, p2, p3, o0, o1, o2, o3):
    row = at_ref[1]
    for k, ref in enumerate((o0, o1, o2, o3)):
        for w in range(3):
            ref[w] = sum(p[w, row ^ k].astype(F32) for p in (p0, p1, p2, p3)).astype(BF)


def joined_sum_kernel(at_ref, p0, p1, p2, p3, o0, o1, o2, o3):
    row = at_ref[1]
    for k, ref in enumerate((o0, o1, o2, o3)):
        ref[...] = sum(p[row ^ k].astype(F32) for p in (p0, p1, p2, p3)).astype(BF)


def row_sum_kernel(at_ref, j0, j1, j2, j3, f0, f1, f2, f3, out_ref):
    row = at_ref[1]
    block = j0.shape[1] // 3
    same = j0[...].astype(F32) + j2[...].astype(F32)
    cross = j1[...].astype(F32) + j3[...].astype(F32)
    low = jnp.where(row % 2 == 0, same, cross)
    high = jnp.where(row % 2 == 0, cross, same)
    parts = []
    for n in range(3):
        parts += [low[:, n * block : (n + 1) * block], high[:, n * block : (n + 1) * block]]
    joined = 6 * block
    out_ref[:, :joined] = jnp.concatenate(parts, axis=1).astype(BF)
    half = f0.shape[2]
    for w in range(3):
        out_ref[:, pl.ds(joined + w * half, half)] = sum(f[w].astype(F32) for f in (f0, f1, f2, f3)).astype(BF)


def weights_kernel(at_ref, p0, p1, p2, p3, q_ref, k_ref, v_ref, h_ref, o_ref, f_ref, turn_s):
    dp = at_ref[0]
    feat, half = q_ref.shape
    quarter = feat // 4
    for n, ref in enumerate((q_ref, k_ref, v_ref, h_ref)):
        for m, part in enumerate((p0, p1, p2, p3)):
            ref[ds16((dp ^ m) * quarter, quarter), :] = part[:, pl.ds(n * half, half)].astype(F32)
    for n, ref in ((4, o_ref), (5, f_ref)):
        for m, part in enumerate((p0, p1, p2, p3)):
            turn_s[ds16((dp ^ m) * quarter, quarter), :] = part[:, pl.ds(n * half, half)].astype(F32)
        ref[...] = turn_s[...].T


def xor_send(value, axis, k, count=4):
    return lax.ppermute(value, axis, [(i, i ^ k) for i in range(count)])


def pair_send(value, k):
    perm = [((r ^ k) * 2 + c, r * 2 + c) for c in range(2) for r in (2 * c, 2 * c + 1)]
    return lax.ppermute(value, RC, perm)


def spot_send(value, k):
    return lax.ppermute(value, RC, [(f, f ^ k) for f in range(8)])


def feature_send(value, k):
    return lax.ppermute(value, RC, [(p * 4 + h, (h ^ k) * 2 + p) for p in range(2) for h in range(4)])


def shards_four(
    tokens_in, segments, query_weight, key_weight, value_weight, output_weight, hidden_weight, hidden_bias,
    final_weight, final_bias, attention_gain, feed_gain, query_scale, clip_limit, cotangent,
):
    feat, seq_len = tokens_in.shape
    width = 4 * feat
    head_dim = query_scale.shape[0]
    half = query_weight.shape[1]
    block = half // 2
    heads = block // head_dim
    toks = seq_len // 4
    quarter = feat // 4
    dp_at, row_at, col_at = lax.axis_index("dp"), lax.axis_index("rows"), lax.axis_index("cols")
    pair = row_at // 2
    spot = (row_at % 2) * 2 + col_at
    here = jnp.stack([dp_at, row_at, col_at]).astype(jnp.int32)
    joined = 3 * block
    padded = -(-(joined + 9) // 128) * 128

    even, odd, feed_own, g_even, g_odd = local_call(
        pack_kernel,
        [((quarter, padded), BF), ((quarter, padded), BF), ((3, quarter, half), BF), ((feat, seq_len // 2), BF), ((feat, seq_len // 2), BF)],
        [pltpu.VMEM((feat, padded - joined), F32), pltpu.VMEM((feat, half), BF)],
        "pack",
        operands=11,
    )(
        here, query_weight, key_weight, value_weight, hidden_weight, output_weight, final_weight,
        attention_gain[None], feed_gain[None], final_bias[None], cotangent,
    )
    joined_parts = [even] + [xor_send(odd if k % 2 else even, "rows", k) for k in range(1, 4)]
    joined_quarter = jnp.stack(joined_parts)
    joined_all = [joined_quarter] + [xor_send(joined_quarter, "dp", m) for m in range(1, 4)]
    x_parts = [tokens_in] + [pair_send(tokens_in, k) for k in range(1, 4)]
    x_other = [swap_cols(x) for x in x_parts]
    feed_parts = [feed_own] + [xor_send(feed_own, "rows", k) for k in range(1, 4)]
    feed_quarter = jnp.stack(feed_parts)
    feed_all = [feed_quarter] + [xor_send(feed_quarter, "dp", m) for m in range(1, 4)]
    feed_other = [swap_cols(w) for w in feed_all]
    g_parts = [g_even] + [pair_send(g_odd if k % 2 else g_even, k) for k in range(1, 4)]
    g_other = [swap_cols(g) for g in g_parts]
    bias_pair = jnp.stack([hidden_bias, swap_cols(hidden_bias)])
    bias_row = jnp.where(col_at == 0, bias_pair, bias_pair[::-1]).reshape(1, 2 * half)

    scale_col = (LOG2E / math.sqrt(head_dim) * jax.nn.softplus(query_scale))[:, None]
    qkv, raw, normed, weight_all, columns, x_tok, inv_tok = local_call(
        project_kernel,
        [
            ((4, joined, toks), BF), ((4, block, toks), F32), ((width, seq_len), BF), ((width, padded), BF),
            ((width, 128), F32), ((width, toks), BF), ((1, toks), F32),
        ],
        [pltpu.VMEM((width, seq_len), BF), pltpu.VMEM((joined, width), BF)],
        "project",
        flops=2 * joined * width * seq_len,
        operands=14,
    )(here, *x_parts, *x_other, *joined_all, scale_col)

    reach = (toks - 1 + PATCH - 1) // toks
    seg_own = lax.dynamic_index_in_dim(segments, pair, 0, keepdims=False)
    seg_row, seg_col = seg_own.reshape(4, 1, toks), seg_own[:, None]
    smem = pl.BlockSpec(memory_space=pltpu.SMEM)
    whole = pl.BlockSpec((4, 1, toks), lambda h: (0, 0, 0))
    column = pl.BlockSpec((seq_len, 1), lambda h: (0, 0))
    single = pl.BlockSpec((head_dim, toks), lambda h: (h, 0))
    stat = pl.BlockSpec((1, 4, 1, toks), lambda h: (h, 0, 0, 0))
    stat_shape = jax.ShapeDtypeStruct((heads, 4, 1, toks), F32)
    act_shape = jax.ShapeDtypeStruct((4, block, toks), BF)
    part_shape = jax.ShapeDtypeStruct((block, toks), BF)
    bias_scratch = pltpu.VMEM((4, min(4, 1 + reach) * toks, toks), F32)
    params = pltpu.CompilerParams(vmem_limit_bytes=60000 * 1024)
    unit = heads * seq_len * seq_len

    def head(offset):
        return pl.BlockSpec((4, head_dim, toks), lambda h: (0, offset * heads + h, 0))

    mixed_all, *mixed_parts, lse, tops = pl.pallas_call(
        functools.partial(attend_fast_kernel, 4, toks, reach),
        grid=(heads,),
        in_specs=[smem, whole, column, head(0), head(1), head(2)],
        out_specs=[head(0), single, single, single, single, stat, stat],
        out_shape=[act_shape] + [part_shape] * 4 + [stat_shape, stat_shape],
        scratch_shapes=[bias_scratch],
        compiler_params=params,
        cost_estimate=pl.CostEstimate(flops=unit * 1024, transcendentals=unit, bytes_accessed=1 << 22),
        name="attend",
    )(here, seg_row, seg_col, qkv, qkv, qkv)

    mixed_parts = [mixed_parts[0]] + [spot_send(mixed_parts[k], k) for k in range(1, 4)]
    out_shape = ((feat, toks), BF)
    *results, rest, common, keep, send, sums = local_call(
        middle_kernel,
        [out_shape] * 8
        + [((width, toks), F32), ((3 * width, toks), BF), ((3 * half, toks), BF), ((3 * half, toks), BF), ((width, 128), F32)],
        [pltpu.VMEM((3, width, 2 * half), BF)]
        + [pltpu.VMEM((width, toks), BF)] * 5
        + [pltpu.SemaphoreType.DMA((96,))],
        "middle",
        flops=12 * width * width * toks,
        operands=24,
        spaces={i: pl.ANY for i in range(16, 24)},
    )(here, x_tok, *mixed_parts, *g_parts, *g_other, columns, bias_row, *feed_all, *feed_other)
    y_parts, mix_parts = results[:4], results[4:]
    mix_parts = [mix_parts[0]] + [spot_send(mix_parts[k], k) for k in range(1, 4)]

    dq, dk, dv, scale_part = pl.pallas_call(
        functools.partial(attend_back_fast_kernel, 4, toks, reach),
        grid=(heads,),
        in_specs=[smem, whole, column, head(0), head(1), head(2), single, single, single, single, head(0), stat, head(0),
                  pl.BlockSpec((head_dim, 1), lambda h: (0, 0))],
        out_specs=[head(0), head(0), head(0), pl.BlockSpec((1, head_dim, toks), lambda h: (h, 0, 0))],
        out_shape=[act_shape, act_shape, act_shape, jax.ShapeDtypeStruct((heads, head_dim, toks), F32)],
        scratch_shapes=[bias_scratch, pltpu.VMEM((4, head_dim, toks), F32), pltpu.VMEM((4, head_dim, toks), F32),
                        pltpu.VMEM((4, head_dim, toks), BF)],
        compiler_params=params,
        cost_estimate=pl.CostEstimate(flops=unit * 2560, transcendentals=unit, bytes_accessed=1 << 23),
        name="attend_back",
    )(here, seg_row, seg_col, qkv, qkv, qkv, *mix_parts, mixed_all, lse, raw, scale_col)

    give_far, give_near, keep_far, keep_near = local_call(
        spread_kernel,
        [((width, toks), BF)] * 4,
        [pltpu.VMEM((joined, toks), BF)],
        "spread",
        flops=2 * joined * width * seq_len,
        operands=5,
    )(here, weight_all, dq, dk, dv)
    chip_far = (keep_far.astype(F32) + swap_cols(give_far).astype(F32)).astype(BF)
    far = xor_send(chip_far, "rows", 1)
    chip_near = swap_cols(give_near)
    *dx_parts, sums_one = local_call(
        input_kernel,
        [out_shape] * 4 + [((width, 128), F32)],
        [pltpu.VMEM((width, toks), BF)],
        "input",
        operands=8,
    )(here, keep_near, chip_near, far, x_tok, inv_tok, rest, columns)

    def to_features(parts, kind):
        parts = [feature_send(part, k) for k, part in enumerate(parts)]
        return local_call(place_kernel, [((feat, seq_len), kind)], [], "place", operands=5)(here, *parts)[0]

    layer_output = to_features(y_parts, BF)
    input_gradient = to_features(dx_parts, F32)

    feed_grads = local_call(
        feed_kernel,
        [((3, 4, quarter, half), BF)] * 4,
        [pltpu.VMEM((width, 2 * toks), BF), pltpu.VMEM((half, 2 * toks), BF), pltpu.VMEM((width, half), BF)],
        "feed",
        flops=12 * width * half * toks,
        operands=5,
    )(here, common, swap_cols(common), keep, swap_cols(send))
    feed_grads = [feed_grads[0]] + [xor_send(feed_grads[k], "dp", k) for k in range(1, 4)]
    feed_rows = local_call(feed_sum_kernel, [((3, quarter, half), BF)] * 4, [], "feed_sum", operands=5)(here, *feed_grads)
    feed_rows = [feed_rows[0]] + [xor_send(feed_rows[k], "rows", k) for k in range(1, 4)]
    joined_grads = local_call(
        joined_kernel,
        [((4, quarter, joined), BF)] * 4,
        [pltpu.VMEM((joined, seq_len), BF), pltpu.VMEM((feat, joined), BF)],
        "joined",
        flops=2 * joined * width * seq_len,
        operands=5,
    )(here, normed, dq, dk, dv)
    joined_grads = [joined_grads[0]] + [xor_send(joined_grads[k], "dp", k) for k in range(1, 4)]
    joined_rows = local_call(joined_sum_kernel, [((quarter, joined), BF)] * 4, [], "joined_sum", operands=5)(here, *joined_grads)
    joined_rows = [joined_rows[0]] + [xor_send(joined_rows[k], "rows", k) for k in range(1, 4)]
    quarter_grads = local_call(row_sum_kernel, [((quarter, 6 * half), BF)], [], "row_sum", operands=9)(
        here, *joined_rows, *feed_rows
    )[0]
    quarter_grads = [quarter_grads] + [xor_send(quarter_grads, "dp", m) for m in range(1, 4)]
    query_grad, key_grad, value_grad, hidden_grad, output_grad, final_grad = local_call(
        weights_kernel,
        [((feat, half), F32)] * 4 + [((half, feat), F32)] * 2,
        [pltpu.VMEM((feat, half), F32)],
        "weights",
        operands=5,
    )(here, *quarter_grads)

    every = (("cols", 2), ("rows", 4), ("dp", 4))
    packed = jnp.concatenate(
        [sums_one[:, 0], sums[:, 0], sums[:, 1], sums[:, 2], jnp.sum(scale_part, axis=(0, 2))]
    )
    head_top = jnp.max(tops, axis=(1, 2, 3))
    tops_all = put(jnp.full((4, heads), NEGATIVE, F32), head_top, col_at * 2 + row_at % 2).reshape(-1)

    def combine(a, b):
        return (a[0] + b[0], jnp.maximum(a[1], b[1]))

    for axis, count in every:
        step = 1
        while step < count:
            joint = xor_send(jnp.concatenate([packed, tops_all]), axis, step, count)
            packed = packed + joint[: packed.shape[0]]
            tops_all = jnp.maximum(tops_all, joint[packed.shape[0] :])
            step *= 2

    def own_block(vector, count, index):
        return pick(vector.reshape(count, -1), index)

    gain_one_sum = own_block(packed[:width], 4, row_at)
    gain_two_sum = own_block(packed[width : 2 * width], 4, row_at)
    bias_one_sum = own_block(packed[2 * width : 3 * width], 2, col_at)
    bias_two_sum = own_block(packed[3 * width : 4 * width], 4, row_at)
    scale_gradient = packed[4 * width :] * (LOG2E / math.sqrt(head_dim)) * jax.nn.sigmoid(query_scale)
    top_heads = own_block(tops_all, 2, col_at)
    factor = jnp.repeat(jnp.sqrt(clip_limit / jnp.maximum(top_heads, clip_limit)), head_dim)
    clipped_query = query_weight.astype(F32) * factor[None, :]
    clipped_key = key_weight.astype(F32) * factor[None, :]
    return (
        layer_output, input_gradient, query_grad, key_grad, value_grad, output_grad, hidden_grad, bias_one_sum,
        final_grad, bias_two_sum, gain_one_sum, gain_two_sum, scale_gradient, top_heads, clipped_query, clipped_key,
    )


def solution(mesh):
    four = mesh.shape["rows"] == 4 and mesh.shape["dp"] == 4
    return jax.shard_map(
        shards_four if four else shards,
        mesh=mesh,
        in_specs=(
            P("rows", ("dp", "cols")),
            P("dp", None),
            P("rows", "cols"),
            P("rows", "cols"),
            P("rows", "cols"),
            P("cols", "rows"),
            P("rows", "cols"),
            P("cols"),
            P("cols", "rows"),
            P("rows"),
            P("rows"),
            P("rows"),
            P(),
            P("cols"),
            P("rows", ("dp", "cols")),
        ),
        out_specs=(
            P("rows", ("dp", "cols")),
            P("rows", ("dp", "cols")),
            P("rows", "cols"),
            P("rows", "cols"),
            P("rows", "cols"),
            P("cols", "rows"),
            P("rows", "cols"),
            P("cols"),
            P("cols", "rows"),
            P("rows"),
            P("rows"),
            P("rows"),
            P(),
            P("cols"),
            P("rows", "cols"),
            P("rows", "cols"),
        ),
        check_vma=False,
    )
```
